32 devices in a mesh: dev: 32 (over z, y, x, core).
Axes of the slice: x: 2, y: 2, z: 4, core: 2. Of those that a mesh axis runs over, the one named last changes fastest.
Arguments:
- factors: bfloat16 [256, 192, 256], P('dev'), may hold values from -6 to 6
- orbital_owner: int32 [256], replicated, may hold values from 0 to 31, as said below
- tile_orbitals: int32 [256, 7], P('dev'), may hold values from 0 to 255, as said below
- projectors: bfloat16 [3072, 192, 128], P('dev'), may hold values from -0.4375 to 0.4375
- amplitudes: float32 [3072, 128, 128], P('dev'), may hold values from -0.3125 to 0.3125
- ranks: int32 [3072], P('dev'), may hold values from 32 to 128, as said below
- pair_energies: float32 [3072, 128], P('dev'), may hold values from 0.5 to 4
- orbital_energies: float32 [256], replicated, may hold values from 0.25 to 2
Outputs:
- new_amplitudes: float32 [3072, 128, 128], P('dev')
- orbital_sums: bfloat16 [256, 192, 256], P('dev')
The draws below stay inside these ranges and needn't reach their ends.
Inputs may be any that keep to these rules, and one draw needn't show every extreme that they name: `orbital_owner`: orbitals o and o + 32 have the same owner, and each device owns 8 orbitals. `tile_orbitals`: rows 8 d to 8 d + 7 are the tiles of device d. A row holds 4 consecutive orbital numbers, then 3 consecutive ones; its 12 pairs are rows 12 t + 3 a + b of the pair arrays. The tiles of one device name no orbital twice, and at most 2 orbitals of one owner; some device reaches 2 in every draw. `ranks`: some pair has rank 128.
All inputs are finite; a program needn't handle non-finite values.
Results may differ from the reference program's by a relative error of at most 0.007.
Values may be sent and summed in bfloat16 or wider, within the bound.
A program may use at most 128 MiB of HBM per device.

```python
import math
import jax
import jax.numpy as jnp
from jax import lax

NAUX = 256
NV = 192
R = 128
ORB_DEV = 8
TILES_DEV = 8
NO = 256
TILES = 256
PAIRS_DEV = 96
PAIRS = 3072
N_DEV = 32


def draw_orbital_owner(key, part):
    owner_perm = jax.random.permutation(jax.random.fold_in(key, 11), N_DEV)
    return owner_perm[jnp.arange(NO) % N_DEV].astype(jnp.int32)


def draw_tile_orbitals(key, part):
    positions = N_DEV // 8
    offsets = jax.random.randint(jax.random.fold_in(key, 21), (N_DEV,), 0, positions)
    level_base_i = jax.random.randint(jax.random.fold_in(key, 22), (N_DEV,), 0, ORB_DEV)
    level_base_j = jax.random.randint(jax.random.fold_in(key, 23), (N_DEV,), 0, ORB_DEV)
    tile_local = jnp.arange(TILES_DEV)
    block_pos = (tile_local[None, :] + offsets[:, None]) % positions
    level_shift = tile_local[None, :] // positions
    level_i = (level_base_i[:, None] + level_shift) % ORB_DEV
    level_j = (level_base_j[:, None] + level_shift) % ORB_DEV
    block_start = 8 * block_pos
    orbits_i = block_start[:, :, None] + jnp.arange(4)[None, None, :] + N_DEV * level_i[:, :, None]
    orbits_j = block_start[:, :, None] + 4 + jnp.arange(3)[None, None, :] + N_DEV * level_j[:, :, None]
    return jnp.concatenate([orbits_i, orbits_j], axis=2).reshape(TILES, 7).astype(jnp.int32)


def draw_ranks(key, part):
    rank_low = R // 4
    rank_upper = jax.random.randint(jax.random.fold_in(key, 31), (N_DEV,), rank_low, R + 1)
    raw_bits = jax.random.randint(jax.random.fold_in(key, 32), (PAIRS,), 0, 1 << 20)
    device_of = jnp.arange(PAIRS) // PAIRS_DEV
    ranks_drawn = rank_low + raw_bits % (rank_upper[device_of] - rank_low + 1)
    chosen = jax.random.randint(jax.random.fold_in(key, 33), (), 0, PAIRS)
    return jnp.where(jnp.arange(PAIRS) == chosen, R, ranks_drawn).astype(jnp.int32)


def shard_levels(rng, shape, split, least, high):
    level, own = 1.0, jax.random.fold_in(rng, 6)
    for axis_at, parts in split:
        draws = jnp.exp(jax.random.uniform(jax.random.fold_in(own, axis_at), (parts,), jnp.float32, least / len(split), high / len(split)))
        level = level * jnp.repeat(draws, shape[axis_at] // parts).reshape([-1 if axis == axis_at else 1 for axis in range(len(shape))])
    return level


def centred(rng, shape, spread, limit, shards=(), held_as=jnp.bfloat16):
    factor_of = shard_levels(rng, shape, shards, -0.22, 0.18) if shards else 1.0
    entries = jax.random.normal(rng, shape, jnp.float32) * spread * factor_of
    return jnp.minimum(jnp.maximum(entries, -limit), limit).astype(held_as)


def setup_inputs(seed: int = 0) -> dict:
    streams_of = jax.random.split(jax.random.key(seed), 9)
    factors = centred(streams_of[0], (NO, NV, NAUX), 0.4, 6.0, ((0, 32),))
    orbital_owner = draw_orbital_owner(jax.random.fold_in(streams_of[8], 71), 0)
    tile_orbitals = draw_tile_orbitals(jax.random.fold_in(streams_of[8], 71), 0)
    projectors = centred(streams_of[3], (PAIRS, NV, R), NV ** -0.5, 0.4375, ((0, 32),))
    amplitudes = centred(streams_of[4], (PAIRS, R, R), 0.02, 0.3125, ((0, 32),), jnp.float32)
    ranks = draw_ranks(jax.random.fold_in(streams_of[8], 71), 0)
    pair_energies = jnp.clip(jnp.exp(math.log(4.0) - 2.0794415 * jax.random.uniform(streams_of[6], (PAIRS, R), jnp.float32) ** shard_levels(streams_of[6], (PAIRS, R), ((0, 32),), -0.2, 0.2)), 0.5, 4.0)
    orbital_energies = jnp.clip(jnp.exp(jax.random.uniform(streams_of[7], (NO,), jnp.float32, math.log(0.25), math.log(2.0))), 0.25, 2.0)
    return {"factors": factors, "orbital_owner": orbital_owner, "tile_orbitals": tile_orbitals, "projectors": projectors, "amplitudes": amplitudes, "ranks": ranks, "pair_energies": pair_energies, "orbital_energies": orbital_energies}


def masked_projectors(projectors, ranks):
    rank_keep = (jnp.arange(R)[None, :] < ranks[:, None]).astype(jnp.bfloat16)
    return projectors * rank_keep[:, None, :]


def tile_projections(rows_i, rows_j, tile_masks):
    masks_float = tile_masks.astype(jnp.float32)
    proj_i = jnp.einsum('avn,abvr->abrn', rows_i.astype(jnp.float32), masks_float).astype(jnp.bfloat16)
    proj_j = jnp.einsum('bvn,abvr->abrn', rows_j.astype(jnp.float32), masks_float).astype(jnp.bfloat16)
    return proj_i, proj_j


def reference(factors, orbital_owner, tile_orbitals, projectors, amplitudes, ranks, pair_energies, orbital_energies):
    storage = (orbital_owner[tile_orbitals] * ORB_DEV + tile_orbitals // N_DEV).astype(jnp.int32)
    masked = masked_projectors(projectors, ranks).reshape(TILES, 4, 3, NV, R)
    amp_half = amplitudes.astype(jnp.bfloat16).reshape(TILES, 4, 3, R, R)

    def accumulate(running, tile_items):
        tile_rows, tile_masks, tile_amps = tile_items
        factor_rows = factors[tile_rows]
        proj_i, proj_j = tile_projections(factor_rows[:4], factor_rows[4:], tile_masks)
        amp_float = tile_amps.astype(jnp.float32)
        cycle_i = jnp.einsum('abrc,abcn->abrn', amp_float, proj_j.astype(jnp.float32)).astype(jnp.bfloat16)
        cycle_j = jnp.einsum('abrc,abrn->abcn', amp_float, proj_i.astype(jnp.float32)).astype(jnp.bfloat16)
        masks_float = tile_masks.astype(jnp.float32)
        sum_i = jnp.einsum('abvr,abrn->avn', masks_float, cycle_i.astype(jnp.float32))
        sum_j = jnp.einsum('abvr,abrn->bvn', masks_float, cycle_j.astype(jnp.float32))
        partial_value = jnp.concatenate([sum_i, sum_j], axis=0).astype(jnp.bfloat16)
        partial_value = lax.optimization_barrier(partial_value).astype(jnp.float32)
        return running.at[tile_rows].add(partial_value), None

    totals, _ = lax.scan(accumulate, jnp.zeros((NO, NV, NAUX), jnp.float32), (storage, masked, amp_half))
    orbital_sums = totals.astype(jnp.bfloat16)
    energy = pair_energies.reshape(TILES, 4, 3, R)
    rank_keep = (jnp.arange(R)[None, :] < ranks[:, None]).astype(jnp.float32).reshape(TILES, 4, 3, R)
    occ_gaps = orbital_energies[tile_orbitals]

    def update(tile_items):
        tile_rows, tile_masks, tile_energy, tile_keep, tile_gaps = tile_items
        factor_rows = factors[tile_rows]
        sum_rows = orbital_sums[tile_rows]
        proj_i, proj_j = tile_projections(factor_rows[:4], factor_rows[4:], tile_masks)
        corr_i, corr_j = tile_projections(sum_rows[:4], sum_rows[4:], tile_masks)
        residual = jnp.einsum('abrn,abcn->abrc', proj_i.astype(jnp.float32), proj_j.astype(jnp.float32))
        residual = residual + jnp.einsum('abrn,abcn->abrc', proj_i.astype(jnp.float32), corr_j.astype(jnp.float32))
        residual = residual + jnp.einsum('abrn,abcn->abrc', corr_i.astype(jnp.float32), proj_j.astype(jnp.float32))
        denominator = tile_energy[:, :, :, None] + tile_energy[:, :, None, :]
        denominator = denominator + tile_gaps[:4, None, None, None] + tile_gaps[None, 4:, None, None]
        return -(tile_keep[:, :, :, None] * tile_keep[:, :, None, :]) * residual / denominator

    updated = lax.map(update, (storage, masked, energy, rank_keep, occ_gaps))
    return updated.reshape(PAIRS, R, R), orbital_sums
```

```python
import jax
import jax.numpy as jnp
from jax import lax
from jax.sharding import PartitionSpec as P


def pack_slots(source_table, slot_rows, slot_valid):
    picked = source_table[slot_rows]
    return jnp.where(slot_valid[:, :, None, None], picked, jnp.zeros_like(picked))


def projections(factor_rows, masked):
    proj_i = jnp.einsum(
        "tavn,tabvr->tabrn", factor_rows[:, :4], masked, preferred_element_type=jnp.float32
    )
    proj_j = jnp.einsum(
        "tbvn,tabvr->tabrn", factor_rows[:, 4:], masked, preferred_element_type=jnp.float32
    )
    return (proj_i.astype(jnp.bfloat16), proj_j.astype(jnp.bfloat16))


GATHER_BYTES = 40 << 20


def slot_body(
    factors,
    orbital_owner,
    tile_orbitals,
    projectors,
    amplitudes,
    ranks,
    pair_energies,
    orbital_energies,
):
    dev_count = lax.axis_size("dev")
    my_index = lax.axis_index("dev")
    tile_count = tile_orbitals.shape[0]
    orb_count = factors.shape[0]
    factor_width = factors.shape[1]
    aux_width = factors.shape[2]
    rank_width = projectors.shape[2]
    need_count = tile_count * 7
    slot_cap = -(-(8 * tile_count) // dev_count)
    my_orbitals = tile_orbitals.reshape(need_count)
    requests = lax.all_gather(my_orbitals, "dev", axis=0, tiled=True).reshape(dev_count, need_count)
    owners = orbital_owner[requests]
    entry_index = jnp.arange(need_count)
    earlier = entry_index[None, :] < entry_index[:, None]
    same_owner = owners[:, :, None] == owners[:, None, :]
    slots = jnp.sum((same_owner & earlier[None]).astype(jnp.int32), axis=2)
    owner_rows = requests // dev_count
    slot_index = jnp.arange(slot_cap)
    send_match = (owners[:, None, :] == my_index) & (slots[:, None, :] == slot_index[None, :, None])
    out_rows = jnp.sum(jnp.where(send_match, owner_rows[:, None, :], 0), axis=2)
    out_valid = jnp.any(send_match, axis=2)
    my_owner = owners[my_index]
    my_slot = slots[my_index]
    arrived = lax.all_to_all(
        pack_slots(factors, out_rows, out_valid), "dev", split_axis=0, concat_axis=0, tiled=True
    )
    fetched = arrived[my_owner, my_slot].reshape(tile_count, 7, factor_width, aux_width)
    rank_keep = jnp.arange(rank_width)[None, :] < ranks[:, None]
    masked = (projectors * rank_keep.astype(jnp.bfloat16)[:, None, :]).reshape(
        tile_count, 4, 3, factor_width, rank_width
    )
    proj_i, proj_j = projections(fetched, masked)
    amp_half = amplitudes.astype(jnp.bfloat16).reshape(tile_count, 4, 3, rank_width, rank_width)
    cycle_i = jnp.einsum(
        "tabrc,tabcn->tabrn", amp_half, proj_j, preferred_element_type=jnp.float32
    ).astype(jnp.bfloat16)
    cycle_j = jnp.einsum(
        "tabrc,tabrn->tabcn", amp_half, proj_i, preferred_element_type=jnp.float32
    ).astype(jnp.bfloat16)
    sum_i = jnp.einsum("tabvr,tabrn->tavn", masked, cycle_i, preferred_element_type=jnp.float32)
    sum_j = jnp.einsum("tabvr,tabrn->tbvn", masked, cycle_j, preferred_element_type=jnp.float32)
    partial_value = (
        jnp.concatenate([sum_i, sum_j], axis=1)
        .astype(jnp.bfloat16)
        .reshape(need_count, factor_width, aux_width)
    )
    peer_index = jnp.arange(dev_count)
    back_match = (my_owner[None, None, :] == peer_index[:, None, None]) & (
        my_slot[None, None, :] == slot_index[None, :, None]
    )
    back_index = jnp.sum(jnp.where(back_match, entry_index[None, None, :], 0), axis=2)
    back_valid = jnp.any(back_match, axis=2)
    outgoing = pack_slots(partial_value, back_index, back_valid)
    selector = (
        (out_rows.reshape(-1)[None, :] == jnp.arange(orb_count)[:, None])
        & out_valid.reshape(-1)[None, :]
    ).astype(jnp.bfloat16)
    incoming = lax.all_to_all(outgoing, "dev", split_axis=0, concat_axis=0, tiled=True)
    totals = jnp.einsum(
        "mq,qvn->mvn",
        selector,
        incoming.reshape(dev_count * slot_cap, factor_width, aux_width),
        preferred_element_type=jnp.float32,
    )
    orbital_sums = totals.astype(jnp.bfloat16)
    returned = lax.all_to_all(
        pack_slots(orbital_sums, out_rows, out_valid),
        "dev",
        split_axis=0,
        concat_axis=0,
        tiled=True,
    )
    collected = returned[my_owner, my_slot].reshape(tile_count, 7, factor_width, aux_width)
    corr_i, corr_j = projections(collected, masked)
    residual = jnp.einsum("tabrn,tabcn->tabrc", proj_i, proj_j, preferred_element_type=jnp.float32)
    residual = residual + jnp.einsum(
        "tabrn,tabcn->tabrc", proj_i, corr_j, preferred_element_type=jnp.float32
    )
    residual = residual + jnp.einsum(
        "tabrn,tabcn->tabrc", corr_i, proj_j, preferred_element_type=jnp.float32
    )
    energy = pair_energies.reshape(tile_count, 4, 3, rank_width)
    occ_gaps = orbital_energies[my_orbitals].reshape(tile_count, 7)
    denominator = energy[:, :, :, :, None] + energy[:, :, :, None, :]
    denominator = (
        denominator + occ_gaps[:, :4, None, None, None] + occ_gaps[:, None, 4:, None, None]
    )
    keep_float = rank_keep.astype(jnp.float32).reshape(tile_count, 4, 3, rank_width)
    updated = (
        -(keep_float[:, :, :, :, None] * keep_float[:, :, :, None, :]) * residual / denominator
    )
    return (updated.reshape(tile_count * 12, rank_width, rank_width), orbital_sums)


def gather_body(
    factors,
    orbital_owner,
    tile_orbitals,
    projectors,
    amplitudes,
    ranks,
    pair_energies,
    orbital_energies,
):
    dev_count = lax.axis_size("dev")
    tile_count = tile_orbitals.shape[0]
    factor_width = factors.shape[1]
    aux_width = factors.shape[2]
    orb_count = factors.shape[0]
    rank_width = projectors.shape[2]
    need_count = tile_count * 7
    my_orbitals = tile_orbitals.reshape(need_count)
    rows = orbital_owner[my_orbitals] * orb_count + my_orbitals // dev_count
    all_factors = lax.all_gather(factors, "dev", axis=0, tiled=True)
    fetched = all_factors[rows].reshape(tile_count, 7, factor_width, aux_width)
    rank_keep = jnp.arange(rank_width)[None, :] < ranks[:, None]
    masked = (projectors * rank_keep.astype(jnp.bfloat16)[:, None, :]).reshape(
        tile_count, 4, 3, factor_width, rank_width
    )
    proj_i, proj_j = projections(fetched, masked)
    amp_half = amplitudes.astype(jnp.bfloat16).reshape(tile_count, 4, 3, rank_width, rank_width)
    cycle_i = jnp.einsum(
        "tabrc,tabcn->tabrn", amp_half, proj_j, preferred_element_type=jnp.float32
    ).astype(jnp.bfloat16)
    cycle_j = jnp.einsum(
        "tabrc,tabrn->tabcn", amp_half, proj_i, preferred_element_type=jnp.float32
    ).astype(jnp.bfloat16)
    sum_i = jnp.einsum("tabvr,tabrn->tavn", masked, cycle_i, preferred_element_type=jnp.float32)
    sum_j = jnp.einsum("tabvr,tabrn->tbvn", masked, cycle_j, preferred_element_type=jnp.float32)
    partial_value = (
        jnp.concatenate([sum_i, sum_j], axis=1)
        .astype(jnp.bfloat16)
        .reshape(need_count, factor_width, aux_width)
    )
    total_rows = dev_count * orb_count
    hit = rows[None, :] == jnp.arange(total_rows)[:, None]
    where_from = jnp.sum(jnp.where(hit, jnp.arange(need_count)[None, :], 0), axis=1)
    named = jnp.any(hit, axis=1)
    dense = jnp.where(
        named[:, None, None], partial_value[where_from], jnp.zeros((), jnp.bfloat16)
    )
    orbital_sums = lax.psum_scatter(dense, "dev", scatter_dimension=0, tiled=True)
    all_sums = lax.all_gather(orbital_sums, "dev", axis=0, tiled=True)
    collected = all_sums[rows].reshape(tile_count, 7, factor_width, aux_width)
    corr_i, corr_j = projections(collected, masked)
    residual = jnp.einsum("tabrn,tabcn->tabrc", proj_i, proj_j, preferred_element_type=jnp.float32)
    residual = residual + jnp.einsum(
        "tabrn,tabcn->tabrc", proj_i, corr_j, preferred_element_type=jnp.float32
    )
    residual = residual + jnp.einsum(
        "tabrn,tabcn->tabrc", corr_i, proj_j, preferred_element_type=jnp.float32
    )
    energy = pair_energies.reshape(tile_count, 4, 3, rank_width)
    occ_gaps = orbital_energies[my_orbitals].reshape(tile_count, 7)
    denominator = energy[:, :, :, :, None] + energy[:, :, :, None, :]
    denominator = (
        denominator + occ_gaps[:, :4, None, None, None] + occ_gaps[:, None, 4:, None, None]
    )
    keep_float = rank_keep.astype(jnp.float32).reshape(tile_count, 4, 3, rank_width)
    updated = (
        -(keep_float[:, :, :, :, None] * keep_float[:, :, :, None, :]) * residual / denominator
    )
    return (updated.reshape(tile_count * 12, rank_width, rank_width), orbital_sums)


def body(factors, *rest):
    gathered = lax.axis_size("dev") * factors.size * factors.dtype.itemsize
    return (gather_body if gathered <= GATHER_BYTES else slot_body)(factors, *rest)


def solution(mesh):
    in_specs = (
        P("dev", None, None),
        P(),
        P("dev", None),
        P("dev", None, None),
        P("dev", None, None),
        P("dev"),
        P("dev", None),
        P(),
    )
    out_specs = (P("dev", None, None), P("dev", None, None))
    return jax.shard_map(body, mesh=mesh, in_specs=in_specs, out_specs=out_specs, check_vma=False)
```

```python
import functools
import math
import jax
import jax.numpy as jnp
from jax import lax
from jax.experimental import pallas as pl
from jax.experimental.pallas import tpu as pltpu
from jax.sharding import PartitionSpec as P

PLANES = 4
MESH = pl.DeviceIdType.MESH
VMEM_LIMIT = 60 << 20


def planes_of(dev_count):
    return math.gcd(PLANES, dev_count)


def place(planes):
    width = lax.axis_size("dev") // planes
    me = lax.axis_index("dev")
    return me, lax.div(me, width), lax.rem(me, width), width


def greet(barrier, me, z, col, planes, width, lines):
    base = z * width

    @pl.loop(1, width)
    def _(step):
        peer = base + lax.rem(col + step, width)
        pl.semaphore_signal(barrier, inc=1, device_id=(peer,), device_id_type=MESH)

    count = width - 1
    if lines:

        @pl.when(z > 0)
        def _():
            pl.semaphore_signal(barrier, inc=1, device_id=(me - width,), device_id_type=MESH)

        @pl.when(z < planes - 1)
        def _():
            pl.semaphore_signal(barrier, inc=1, device_id=(me + width,), device_id_type=MESH)

        count = count + jnp.where(z > 0, 1, 0) + jnp.where(z < planes - 1, 1, 0)

    pl.semaphore_wait(barrier, count)


def ask_kernel(planes, want, got, send, recv):
    me, z, col, width = place(planes)
    greet(pltpu.get_barrier_semaphore(), me, z, col, planes, width, False)

    def copy_to(peer):
        return pltpu.make_async_remote_copy(
            src_ref=want.at[peer],
            dst_ref=got.at[col],
            send_sem=send.at[peer],
            recv_sem=recv.at[col],
            device_id=(z * width + peer,),
            device_id_type=MESH,
        )

    def arrival(peer):
        return pltpu.make_async_remote_copy(
            src_ref=want.at[peer],
            dst_ref=got.at[peer],
            send_sem=send.at[peer],
            recv_sem=recv.at[peer],
            device_id=(z * width + peer,),
            device_id_type=MESH,
        )

    @pl.loop(1, width)
    def _(step):
        copy_to(lax.rem(col + step, width)).start()

    got[col] = want[col]

    @pl.loop(1, width)
    def _(step):
        peer = lax.rem(col + step, width)
        arrival(peer).wait_recv()
        arrival(peer).wait_send()


def ask(want, planes):
    width = want.shape[0]
    return pl.pallas_call(
        functools.partial(ask_kernel, planes),
        out_shape=jax.ShapeDtypeStruct(want.shape, want.dtype),
        in_specs=[pl.BlockSpec(memory_space=pltpu.VMEM)],
        out_specs=pl.BlockSpec(memory_space=pltpu.VMEM),
        scratch_shapes=[pltpu.SemaphoreType.DMA((width,)), pltpu.SemaphoreType.DMA((width,))],
        compiler_params=pltpu.CompilerParams(collective_id=1, has_side_effects=True),
        name="ask",
    )(want)


def fetch_kernel(planes, slots, picks, source, out, mine, *scratch):
    below, above = scratch[: planes - 1], scratch[planes - 1 : 2 * planes - 2]
    pack, local, line_send, line_recv, send, recv, keep = scratch[2 * planes - 2 :]
    me, z, col, width = place(planes)
    greet(pltpu.get_barrier_semaphore(), me, z, col, planes, width, True)
    load = pltpu.make_async_copy(source, mine, local.at[0])
    load.start()

    def hop(way, dist):
        held = below if way == 0 else above
        return pltpu.make_async_remote_copy(
            src_ref=source if dist == 0 else held[dist - 1],
            dst_ref=held[dist],
            send_sem=line_send.at[way, dist],
            recv_sem=line_recv.at[way, dist],
            device_id=(me + width if way == 0 else me - width,),
            device_id_type=MESH,
        )

    def onward(way):
        return z < planes - 1 if way == 0 else z > 0

    def there(way, dist):
        return z - dist >= 0 if way == 0 else z + dist < planes

    def sent(peer, block, home):
        span = pl.ds(block * slots, slots)
        return pltpu.make_async_remote_copy(
            src_ref=pack.at[peer, span],
            dst_ref=out.at[home, span],
            send_sem=send.at[peer, block],
            recv_sem=recv.at[home, block],
            device_id=(z * width + peer,),
            device_id_type=MESH,
        )

    def kept(block):
        span = pl.ds(block * slots, slots)
        return pltpu.make_async_copy(pack.at[col, span], out.at[col, span], keep.at[block])

    def serve(held, block):
        @pl.loop(0, width)
        def _(step):
            peer = lax.rem(col + step, width)
            for slot in range(slots):
                at = block * slots + slot
                pack[peer, at] = held[picks[peer, at]]

        @pl.loop(1, width)
        def _(step):
            sent(lax.rem(col + step, width), block, col).start()

        kept(block).start()

    for way in range(2):
        if planes > 1:

            @pl.when(onward(way))
            def _():
                hop(way, 0).start()

    load.wait()
    serve(mine, z)
    for dist in range(1, planes):
        for way in range(2):

            @pl.when(there(way, dist))
            def _():
                hop(way, dist - 1).wait_recv()
                if dist < planes - 1:

                    @pl.when(onward(way))
                    def _():
                        hop(way, dist).start()

                serve((below if way == 0 else above)[dist - 1], z - dist if way == 0 else z + dist)

    for dist in range(planes - 1):
        for way in range(2):

            @pl.when(onward(way) & there(way, dist))
            def _():
                hop(way, dist).wait_send()

    @pl.loop(0, planes)
    def _(block):
        @pl.loop(1, width)
        def _(step):
            peer = lax.rem(col + step, width)
            sent(peer, block, peer).wait_recv()
            sent(peer, block, peer).wait_send()

        kept(block).wait()


def fetch(source, picks, planes, slots, ident):
    width = picks.shape[0]
    held = pltpu.VMEM(source.shape, source.dtype)
    slab = source.shape[1:]
    return pl.pallas_call(
        functools.partial(fetch_kernel, planes, slots),
        out_shape=jax.ShapeDtypeStruct((width, planes * slots) + slab, source.dtype),
        in_specs=[
            pl.BlockSpec(memory_space=pltpu.SMEM),
            pl.BlockSpec(memory_space=pl.ANY),
        ],
        out_specs=pl.BlockSpec(memory_space=pl.ANY),
        scratch_shapes=[held]
        + [held] * (2 * planes - 2)
        + [
            pltpu.VMEM((width, planes * slots) + slab, source.dtype),
            pltpu.SemaphoreType.DMA((1,)),
            pltpu.SemaphoreType.DMA((2, planes)),
            pltpu.SemaphoreType.DMA((2, planes)),
            pltpu.SemaphoreType.DMA((width, planes)),
            pltpu.SemaphoreType.DMA((width, planes)),
            pltpu.SemaphoreType.DMA((planes,)),
        ],
        compiler_params=pltpu.CompilerParams(
            collective_id=ident, has_side_effects=True, vmem_limit_bytes=VMEM_LIMIT
        ),
        name=f"fetch_{ident}",
    )(picks, source)


def farthest_first(planes, z, turn):
    block = 0
    for own in range(planes):
        order = sorted(range(planes), key=lambda b: (-abs(b - own), b))
        block = block + jnp.where(z == own, order[turn], 0)
    return block


def row_chunk(rows):
    return next(size for size in (64, 48, 32, 16, 8, rows) if rows % size == 0)


def reduce_kernel(planes, slots, table, outgoing, out, *scratch):
    landed = scratch[:planes]
    total, inbox, outbox, send, recv, keep, line_send, line_recv = scratch[planes:]
    me, z, col, width = place(planes)
    orbs, rows = total.shape[:2]
    chunk = row_chunk(rows)
    greet(pltpu.get_barrier_semaphore(), me, z, col, planes, width, True)

    def sent(peer, turn, home):
        span = pl.ds(farthest_first(planes, z, turn) * slots, slots)
        return pltpu.make_async_remote_copy(
            src_ref=outgoing.at[peer, span],
            dst_ref=landed[turn].at[pl.ds(home * slots, slots)],
            send_sem=send.at[peer, turn],
            recv_sem=recv.at[home, turn],
            device_id=(z * width + peer,),
            device_id_type=MESH,
        )

    def kept(turn):
        span = pl.ds(farthest_first(planes, z, turn) * slots, slots)
        return pltpu.make_async_copy(
            outgoing.at[col, span], landed[turn].at[pl.ds(col * slots, slots)], keep.at[turn]
        )

    def hop(way, block):
        return pltpu.make_async_remote_copy(
            src_ref=outbox.at[block],
            dst_ref=inbox.at[way, block],
            send_sem=line_send.at[block],
            recv_sem=line_recv.at[way, block],
            device_id=(me + width if way == 0 else me - width,),
            device_id_type=MESH,
        )

    for turn in range(planes):

        @pl.loop(1, width)
        def _(step):
            sent(lax.rem(col + step, width), turn, col).start()

        kept(turn).start()

    def add_line(way, block):
        hop(way, block).wait_recv()

        @pl.loop(0, orbs)
        def _(orb):
            for first in range(0, rows, chunk):
                part = pl.ds(first, chunk)
                total[orb, part] += inbox[way, block, orb, part].astype(jnp.float32)

    for turn in range(planes):
        block = farthest_first(planes, z, turn)

        @pl.loop(1, width)
        def _(step):
            peer = lax.rem(col + step, width)
            sent(peer, turn, peer).wait_recv()

        kept(turn).wait()

        @pl.loop(0, orbs)
        def _(orb):
            for first in range(0, rows, chunk):
                part = pl.ds(first, chunk)
                value = jnp.zeros((chunk, total.shape[2]), jnp.float32)
                for source in range(width):
                    at = table[block * orbs + orb, source]
                    slab = landed[turn][jnp.maximum(at, 0), part].astype(jnp.float32)
                    value = value + jnp.where(at >= 0, slab, 0.0)
                total[orb, part] = value

        if turn < planes - 1:
            for way in range(2):

                @pl.when(block > z if way == 0 else block < z)
                def _():
                    @pl.when(z > 0 if way == 0 else z < planes - 1)
                    def _():
                        add_line(way, block)

                    outbox[block] = total[...].astype(outbox.dtype)
                    hop(way, block).start()

        else:

            @pl.when(z > 0)
            def _():
                add_line(0, z)

            @pl.when(z < planes - 1)
            def _():
                add_line(1, z)

            out[...] = total[...].astype(out.dtype)

    for turn in range(planes):
        if turn < planes - 1:
            hop(0, farthest_first(planes, z, turn)).wait_send()

        @pl.loop(1, width)
        def _(step):
            sent(lax.rem(col + step, width), turn, col).wait_send()


def reduce_slots(outgoing, table, orbs, planes, slots):
    width = outgoing.shape[0]
    slab = outgoing.shape[2:]
    kind = outgoing.dtype
    return pl.pallas_call(
        functools.partial(reduce_kernel, planes, slots),
        out_shape=jax.ShapeDtypeStruct((orbs,) + slab, kind),
        in_specs=[
            pl.BlockSpec(memory_space=pltpu.SMEM),
            pl.BlockSpec(memory_space=pl.ANY),
        ],
        out_specs=pl.BlockSpec(memory_space=pltpu.VMEM),
        scratch_shapes=[pltpu.VMEM((width * slots,) + slab, kind)] * planes
        + [
            pltpu.VMEM((orbs,) + slab, jnp.float32),
            pltpu.VMEM((2, planes, orbs) + slab, kind),
            pltpu.VMEM((planes, orbs) + slab, kind),
            pltpu.SemaphoreType.DMA((width, planes)),
            pltpu.SemaphoreType.DMA((width, planes)),
            pltpu.SemaphoreType.DMA((planes,)),
            pltpu.SemaphoreType.DMA((planes,)),
            pltpu.SemaphoreType.DMA((2, planes)),
        ],
        compiler_params=pltpu.CompilerParams(
            collective_id=3, has_side_effects=True, vmem_limit_bytes=VMEM_LIMIT
        ),
        name="reduce_slots",
    )(table, outgoing)


def projections(factor_rows, masked):
    proj_i = jnp.einsum(
        "tavn,tabvr->tabrn", factor_rows[:, :4], masked, preferred_element_type=jnp.float32
    )
    proj_j = jnp.einsum(
        "tbvn,tabvr->tabrn", factor_rows[:, 4:], masked, preferred_element_type=jnp.float32
    )
    return (proj_i.astype(jnp.bfloat16), proj_j.astype(jnp.bfloat16))


def body(
    factors,
    orbital_owner,
    tile_orbitals,
    projectors,
    amplitudes,
    ranks,
    pair_energies,
    orbital_energies,
):
    dev_count = lax.axis_size("dev")
    planes = planes_of(dev_count)
    width = dev_count // planes
    tile_count = tile_orbitals.shape[0]
    orb_count, factor_width, aux_width = factors.shape
    rank_width = projectors.shape[2]
    need_count = tile_count * 7
    slots = -(-(8 * tile_count) // dev_count)
    my_orbitals = tile_orbitals.reshape(need_count)
    owner = orbital_owner[my_orbitals]
    entry = jnp.arange(need_count)
    same = (owner[:, None] == owner[None, :]) & (entry[None, :] < entry[:, None])
    slot = jnp.sum(same.astype(jnp.int32), axis=1)
    spot = lax.rem(owner, width) * (planes * slots) + lax.div(owner, width) * slots + slot
    hit = spot[None, :] == jnp.arange(dev_count * slots)[:, None]
    entry_at = jnp.sum(jnp.where(hit, entry[None, :], 0), axis=1)
    row_at = jnp.sum(jnp.where(hit, lax.div(my_orbitals, dev_count)[None, :] + 1, 0), axis=1) - 1
    want = jnp.zeros((width, 8, 128), jnp.int32)
    want = want.at[:, 0, : planes * slots].set(row_at.reshape(width, planes * slots))
    asked = ask(want, planes)[:, 0, : planes * slots]
    picks = jnp.maximum(asked, 0)
    by_plane = asked.reshape(width, planes, slots).transpose(1, 0, 2)
    match = by_plane[:, None] == jnp.arange(orb_count)[None, :, None, None]
    slot_code = jnp.arange(width * slots).reshape(width, slots)
    table = jnp.sum(jnp.where(match, slot_code + 1, 0), axis=3) - 1
    table = table.reshape(planes * orb_count, width)
    arrived = fetch(factors, picks, planes, slots, 2)
    arrived = arrived.reshape(dev_count * slots, factor_width, aux_width)
    fetched = arrived[spot].reshape(tile_count, 7, factor_width, aux_width)
    rank_keep = jnp.arange(rank_width)[None, :] < ranks[:, None]
    masked = (projectors * rank_keep.astype(jnp.bfloat16)[:, None, :]).reshape(
        tile_count, 4, 3, factor_width, rank_width
    )
    proj_i, proj_j = projections(fetched, masked)
    amp_half = amplitudes.astype(jnp.bfloat16).reshape(tile_count, 4, 3, rank_width, rank_width)
    cycle_i = jnp.einsum(
        "tabrc,tabcn->tabrn", amp_half, proj_j, preferred_element_type=jnp.float32
    ).astype(jnp.bfloat16)
    cycle_j = jnp.einsum(
        "tabrc,tabrn->tabcn", amp_half, proj_i, preferred_element_type=jnp.float32
    ).astype(jnp.bfloat16)
    sum_i = jnp.einsum("tabvr,tabrn->tavn", masked, cycle_i, preferred_element_type=jnp.float32)
    sum_j = jnp.einsum("tabvr,tabrn->tbvn", masked, cycle_j, preferred_element_type=jnp.float32)
    partial_value = (
        jnp.concatenate([sum_i, sum_j], axis=1)
        .astype(jnp.bfloat16)
        .reshape(need_count, factor_width, aux_width)
    )
    outgoing = partial_value[entry_at].reshape(width, planes * slots, factor_width, aux_width)
    orbital_sums = reduce_slots(outgoing, table, orb_count, planes, slots)
    returned = fetch(orbital_sums, picks, planes, slots, 4)
    returned = returned.reshape(dev_count * slots, factor_width, aux_width)
    collected = returned[spot].reshape(tile_count, 7, factor_width, aux_width)
    corr_i, corr_j = projections(collected, masked)
    residual = jnp.einsum("tabrn,tabcn->tabrc", proj_i, proj_j, preferred_element_type=jnp.float32)
    residual = residual + jnp.einsum(
        "tabrn,tabcn->tabrc", proj_i, corr_j, preferred_element_type=jnp.float32
    )
    residual = residual + jnp.einsum(
        "tabrn,tabcn->tabrc", corr_i, proj_j, preferred_element_type=jnp.float32
    )
    energy = pair_energies.reshape(tile_count, 4, 3, rank_width)
    occ_gaps = orbital_energies[my_orbitals].reshape(tile_count, 7)
    denominator = energy[:, :, :, :, None] + energy[:, :, :, None, :]
    denominator = (
        denominator + occ_gaps[:, :4, None, None, None] + occ_gaps[:, None, 4:, None, None]
    )
    keep_float = rank_keep.astype(jnp.float32).reshape(tile_count, 4, 3, rank_width)
    updated = (
        -(keep_float[:, :, :, :, None] * keep_float[:, :, :, None, :]) * residual / denominator
    )
    return (updated.reshape(tile_count * 12, rank_width, rank_width), orbital_sums)


def solution(mesh):
    in_specs = (
        P("dev", None, None),
        P(),
        P("dev", None),
        P("dev", None, None),
        P("dev", None, None),
        P("dev"),
        P("dev", None),
        P(),
    )
    out_specs = (P("dev", None, None), P("dev", None, None))
    return jax.shard_map(body, mesh=mesh, in_specs=in_specs, out_specs=out_specs, check_vma=False)
```

```python
import functools
import math
import jax
import jax.numpy as jnp
from jax import lax
from jax.experimental import pallas as pl
from jax.experimental.pallas import tpu as pltpu
from jax.sharding import PartitionSpec as P

PLANES = 4
MESH = pl.DeviceIdType.MESH
VMEM_LIMIT = 60 << 20


def planes_of(dev_count):
    return math.gcd(PLANES, dev_count)


def place(planes):
    width = lax.axis_size("dev") // planes
    me = lax.axis_index("dev")
    return me, lax.div(me, width), lax.rem(me, width), width


def greet(barrier, me, z, col, planes, width, lines):
    base = z * width

    @pl.loop(1, width)
    def _(step):
        peer = base + lax.rem(col + step, width)
        pl.semaphore_signal(barrier, inc=1, device_id=(peer,), device_id_type=MESH)

    count = width - 1
    if lines:

        @pl.when(z > 0)
        def _():
            pl.semaphore_signal(barrier, inc=1, device_id=(me - width,), device_id_type=MESH)

        @pl.when(z < planes - 1)
        def _():
            pl.semaphore_signal(barrier, inc=1, device_id=(me + width,), device_id_type=MESH)

        count = count + jnp.where(z > 0, 1, 0) + jnp.where(z < planes - 1, 1, 0)

    pl.semaphore_wait(barrier, count)


def ask_kernel(planes, want, got, send, recv):
    me, z, col, width = place(planes)
    greet(pltpu.get_barrier_semaphore(), me, z, col, planes, width, False)

    def copy_to(peer):
        return pltpu.make_async_remote_copy(
            src_ref=want.at[peer],
            dst_ref=got.at[col],
            send_sem=send.at[peer],
            recv_sem=recv.at[col],
            device_id=(z * width + peer,),
            device_id_type=MESH,
        )

    def arrival(peer):
        return pltpu.make_async_remote_copy(
            src_ref=want.at[peer],
            dst_ref=got.at[peer],
            send_sem=send.at[peer],
            recv_sem=recv.at[peer],
            device_id=(z * width + peer,),
            device_id_type=MESH,
        )

    @pl.loop(1, width)
    def _(step):
        copy_to(lax.rem(col + step, width)).start()

    got[col] = want[col]

    @pl.loop(1, width)
    def _(step):
        peer = lax.rem(col + step, width)
        arrival(peer).wait_recv()
        arrival(peer).wait_send()


def ask(want, planes):
    width = want.shape[0]
    return pl.pallas_call(
        functools.partial(ask_kernel, planes),
        out_shape=jax.ShapeDtypeStruct(want.shape, want.dtype),
        in_specs=[pl.BlockSpec(memory_space=pltpu.VMEM)],
        out_specs=pl.BlockSpec(memory_space=pltpu.VMEM),
        scratch_shapes=[pltpu.SemaphoreType.DMA((width,)), pltpu.SemaphoreType.DMA((width,))],
        compiler_params=pltpu.CompilerParams(collective_id=1, has_side_effects=True),
        name="ask",
    )(want)


def fetch_kernel(planes, slots, picks, source, out, mine, *scratch):
    below, above = scratch[: planes - 1], scratch[planes - 1 : 2 * planes - 2]
    pack, local, line_send, line_recv, send, recv, keep = scratch[2 * planes - 2 :]
    me, z, col, width = place(planes)
    greet(pltpu.get_barrier_semaphore(), me, z, col, planes, width, True)
    load = pltpu.make_async_copy(source, mine, local.at[0])
    load.start()

    def hop(way, dist):
        held = below if way == 0 else above
        return pltpu.make_async_remote_copy(
            src_ref=source if dist == 0 else held[dist - 1],
            dst_ref=held[dist],
            send_sem=line_send.at[way, dist],
            recv_sem=line_recv.at[way, dist],
            device_id=(me + width if way == 0 else me - width,),
            device_id_type=MESH,
        )

    def onward(way):
        return z < planes - 1 if way == 0 else z > 0

    def there(way, dist):
        return z - dist >= 0 if way == 0 else z + dist < planes

    def sent(peer, block, home):
        span = pl.ds(block * slots, slots)
        return pltpu.make_async_remote_copy(
            src_ref=pack.at[peer, span],
            dst_ref=out.at[home, span],
            send_sem=send.at[peer, block],
            recv_sem=recv.at[home, block],
            device_id=(z * width + peer,),
            device_id_type=MESH,
        )

    def kept(block):
        span = pl.ds(block * slots, slots)
        return pltpu.make_async_copy(pack.at[col, span], out.at[col, span], keep.at[block])

    def serve(held, block):
        @pl.loop(0, width)
        def _(step):
            peer = lax.rem(col + step, width)
            for slot in range(slots):
                at = block * slots + slot
                pack[peer, at] = held[picks[peer, at]]

        @pl.loop(1, width)
        def _(step):
            sent(lax.rem(col + step, width), block, col).start()

        kept(block).start()

    for way in range(2):
        if planes > 1:

            @pl.when(onward(way))
            def _():
                hop(way, 0).start()

    load.wait()
    serve(mine, z)
    for dist in range(1, planes):
        for way in range(2):

            @pl.when(there(way, dist))
            def _():
                hop(way, dist - 1).wait_recv()
                if dist < planes - 1:

                    @pl.when(onward(way))
                    def _():
                        hop(way, dist).start()

                serve((below if way == 0 else above)[dist - 1], z - dist if way == 0 else z + dist)

    for dist in range(planes - 1):
        for way in range(2):

            @pl.when(onward(way) & there(way, dist))
            def _():
                hop(way, dist).wait_send()

    @pl.loop(0, planes)
    def _(block):
        @pl.loop(1, width)
        def _(step):
            peer = lax.rem(col + step, width)
            sent(peer, block, peer).wait_recv()
            sent(peer, block, peer).wait_send()

        kept(block).wait()


def fetch(source, picks, planes, slots, ident):
    width = picks.shape[0]
    held = pltpu.VMEM(source.shape, source.dtype)
    slab = source.shape[1:]
    return pl.pallas_call(
        functools.partial(fetch_kernel, planes, slots),
        out_shape=jax.ShapeDtypeStruct((width, planes * slots) + slab, source.dtype),
        in_specs=[
            pl.BlockSpec(memory_space=pltpu.SMEM),
            pl.BlockSpec(memory_space=pl.ANY),
        ],
        out_specs=pl.BlockSpec(memory_space=pl.ANY),
        scratch_shapes=[held]
        + [held] * (2 * planes - 2)
        + [
            pltpu.VMEM((width, planes * slots) + slab, source.dtype),
            pltpu.SemaphoreType.DMA((1,)),
            pltpu.SemaphoreType.DMA((2, planes)),
            pltpu.SemaphoreType.DMA((2, planes)),
            pltpu.SemaphoreType.DMA((width, planes)),
            pltpu.SemaphoreType.DMA((width, planes)),
            pltpu.SemaphoreType.DMA((planes,)),
        ],
        compiler_params=pltpu.CompilerParams(
            collective_id=ident, has_side_effects=True, vmem_limit_bytes=VMEM_LIMIT
        ),
        name=f"fetch_{ident}",
    )(picks, source)


def farthest_first(planes, z, turn):
    block = 0
    for own in range(planes):
        order = sorted(range(planes), key=lambda b: (-abs(b - own), b))
        block = block + jnp.where(z == own, order[turn], 0)
    return block


def row_chunk(rows):
    return next(size for size in (64, 48, 32, 16, 8, rows) if rows % size == 0)


def reduce_kernel(planes, slots, table, outgoing, out, *scratch):
    landed = scratch[:planes]
    total, inbox, outbox, send, recv, keep, line_send, line_recv = scratch[planes:]
    me, z, col, width = place(planes)
    orbs, rows = total.shape[:2]
    chunk = row_chunk(rows)
    greet(pltpu.get_barrier_semaphore(), me, z, col, planes, width, True)

    def sent(peer, turn, home):
        span = pl.ds(farthest_first(planes, z, turn) * slots, slots)
        return pltpu.make_async_remote_copy(
            src_ref=outgoing.at[peer, span],
            dst_ref=landed[turn].at[pl.ds(home * slots, slots)],
            send_sem=send.at[peer, turn],
            recv_sem=recv.at[home, turn],
            device_id=(z * width + peer,),
            device_id_type=MESH,
        )

    def kept(turn):
        span = pl.ds(farthest_first(planes, z, turn) * slots, slots)
        return pltpu.make_async_copy(
            outgoing.at[col, span], landed[turn].at[pl.ds(col * slots, slots)], keep.at[turn]
        )

    def hop(way, block):
        return pltpu.make_async_remote_copy(
            src_ref=outbox.at[block],
            dst_ref=inbox.at[way, block],
            send_sem=line_send.at[block],
            recv_sem=line_recv.at[way, block],
            device_id=(me + width if way == 0 else me - width,),
            device_id_type=MESH,
        )

    for turn in range(planes):

        @pl.loop(1, width)
        def _(step):
            sent(lax.rem(col + step, width), turn, col).start()

        kept(turn).start()

    def add_line(way, block):
        hop(way, block).wait_recv()

        @pl.loop(0, orbs)
        def _(orb):
            for first in range(0, rows, chunk):
                part = pl.ds(first, chunk)
                total[orb, part] += inbox[way, block, orb, part].astype(jnp.float32)

    for turn in range(planes):
        block = farthest_first(planes, z, turn)

        @pl.loop(1, width)
        def _(step):
            peer = lax.rem(col + step, width)
            sent(peer, turn, peer).wait_recv()

        kept(turn).wait()

        @pl.loop(0, orbs)
        def _(orb):
            for first in range(0, rows, chunk):
                part = pl.ds(first, chunk)
                value = jnp.zeros((chunk, total.shape[2]), jnp.float32)
                for source in range(width):
                    at = table[block * orbs + orb, source]
                    slab = landed[turn][jnp.maximum(at, 0), part].astype(jnp.float32)
                    value = value + jnp.where(at >= 0, slab, 0.0)
                total[orb, part] = value

        if turn < planes - 1:
            for way in range(2):

                @pl.when(block > z if way == 0 else block < z)
                def _():
                    @pl.when(z > 0 if way == 0 else z < planes - 1)
                    def _():
                        add_line(way, block)

                    outbox[block] = total[...].astype(outbox.dtype)
                    hop(way, block).start()

        else:

            @pl.when(z > 0)
            def _():
                add_line(0, z)

            @pl.when(z < planes - 1)
            def _():
                add_line(1, z)

            out[...] = total[...].astype(out.dtype)

    for turn in range(planes):
        if turn < planes - 1:
            hop(0, farthest_first(planes, z, turn)).wait_send()

        @pl.loop(1, width)
        def _(step):
            sent(lax.rem(col + step, width), turn, col).wait_send()


def reduce_slots(outgoing, table, orbs, planes, slots):
    width = outgoing.shape[0]
    slab = outgoing.shape[2:]
    kind = outgoing.dtype
    return pl.pallas_call(
        functools.partial(reduce_kernel, planes, slots),
        out_shape=jax.ShapeDtypeStruct((orbs,) + slab, kind),
        in_specs=[
            pl.BlockSpec(memory_space=pltpu.SMEM),
            pl.BlockSpec(memory_space=pl.ANY),
        ],
        out_specs=pl.BlockSpec(memory_space=pltpu.VMEM),
        scratch_shapes=[pltpu.VMEM((width * slots,) + slab, kind)] * planes
        + [
            pltpu.VMEM((orbs,) + slab, jnp.float32),
            pltpu.VMEM((2, planes, orbs) + slab, kind),
            pltpu.VMEM((planes, orbs) + slab, kind),
            pltpu.SemaphoreType.DMA((width, planes)),
            pltpu.SemaphoreType.DMA((width, planes)),
            pltpu.SemaphoreType.DMA((planes,)),
            pltpu.SemaphoreType.DMA((planes,)),
            pltpu.SemaphoreType.DMA((2, planes)),
        ],
        compiler_params=pltpu.CompilerParams(
            collective_id=3, has_side_effects=True, vmem_limit_bytes=VMEM_LIMIT
        ),
        name="reduce_slots",
    )(table, outgoing)


LEFT, RIGHT = 4, 3
PAIRS_TILE = LEFT * RIGHT


def masked_blocks(ranks, projectors, tile):
    kept = []
    for pair in range(PAIRS_TILE):
        value = projectors[pair]
        lane = lax.broadcasted_iota(jnp.int32, value.shape, 1)
        kept.append(jnp.where(lane < ranks[tile * PAIRS_TILE + pair], value, jnp.zeros_like(value)))
    return kept


def project(turned, slabs, left_out, right_out):
    width = turned[0].shape[0]
    for a in range(LEFT):
        stack = jnp.concatenate([turned[RIGHT * a + b] for b in range(RIGHT)], axis=0)
        value = jnp.dot(stack, slabs[a][0], preferred_element_type=jnp.float32)
        value = value.astype(left_out.dtype)
        for b in range(RIGHT):
            left_out[RIGHT * a + b] = value[b * width : (b + 1) * width]
    for b in range(RIGHT):
        stack = jnp.concatenate([turned[RIGHT * a + b] for a in range(LEFT)], axis=0)
        value = jnp.dot(stack, slabs[LEFT + b][0], preferred_element_type=jnp.float32)
        value = value.astype(right_out.dtype)
        for a in range(LEFT):
            right_out[RIGHT * a + b] = value[a * width : (a + 1) * width]


def cycle_kernel(spot, ranks, *refs):
    slabs = refs[: LEFT + RIGHT]
    projectors, amplitudes, out, left, right, staged, sems = refs[LEFT + RIGHT :]
    tile = pl.program_id(0)
    half = lax.rem(tile, 2)

    def put(at, which, entry):
        target = out.at[spot[at * (LEFT + RIGHT) + entry]]
        return pltpu.make_async_copy(staged.at[which, entry], target, sems.at[which, entry])

    kept = masked_blocks(ranks, projectors, tile)
    project([value.T for value in kept], slabs, left, right)
    for pair in range(PAIRS_TILE):
        amp = amplitudes[pair].astype(jnp.bfloat16)
        from_right = jnp.dot(amp, right[pair], preferred_element_type=jnp.float32)
        from_left = jnp.dot(amp.T, left[pair], preferred_element_type=jnp.float32)
        left[pair] = from_right.astype(left.dtype)
        right[pair] = from_left.astype(right.dtype)

    @pl.when(tile >= 2)
    def _():
        for entry in range(LEFT + RIGHT):
            put(tile - 2, half, entry).wait()

    for entry in range(LEFT + RIGHT):
        if entry < LEFT:
            pairs, cycles = [RIGHT * entry + b for b in range(RIGHT)], left
        else:
            pairs, cycles = [RIGHT * a + entry - LEFT for a in range(LEFT)], right
        wide = jnp.concatenate([kept[pair] for pair in pairs], axis=1)
        tall = jnp.concatenate([cycles[pair] for pair in pairs], axis=0)
        value = jnp.dot(wide, tall, preferred_element_type=jnp.float32)
        staged[half, entry] = value.astype(staged.dtype)
        put(tile, half, entry).start()

    @pl.when(tile == pl.num_programs(0) - 1)
    def _():
        for entry in range(LEFT + RIGHT):
            put(tile, half, entry).wait()

        @pl.when(tile >= 1)
        def _():
            for entry in range(LEFT + RIGHT):
                put(tile - 1, 1 - half, entry).wait()


def slab_specs(slab):
    def at(entry):
        return lambda tile, spot, *_: (spot[tile * (LEFT + RIGHT) + entry], 0, 0)

    return [pl.BlockSpec((1,) + slab, at(entry)) for entry in range(LEFT + RIGHT)]


def cycles(spot, ranks, arrived, projectors, amplitudes):
    slab = arrived.shape[1:]
    wide = projectors.shape[2]
    held = pltpu.VMEM((PAIRS_TILE, wide, slab[1]), arrived.dtype)
    grid_spec = pltpu.PrefetchScalarGridSpec(
        num_scalar_prefetch=2,
        grid=(projectors.shape[0] // PAIRS_TILE,),
        in_specs=slab_specs(slab)
        + [
            pl.BlockSpec((PAIRS_TILE,) + projectors.shape[1:], lambda tile, *_: (tile, 0, 0)),
            pl.BlockSpec((PAIRS_TILE,) + amplitudes.shape[1:], lambda tile, *_: (tile, 0, 0)),
        ],
        out_specs=pl.BlockSpec(memory_space=pl.ANY),
        scratch_shapes=[
            held,
            held,
            pltpu.VMEM((2, LEFT + RIGHT) + slab, arrived.dtype),
            pltpu.SemaphoreType.DMA((2, LEFT + RIGHT)),
        ],
    )
    return pl.pallas_call(
        cycle_kernel,
        out_shape=jax.ShapeDtypeStruct(arrived.shape, arrived.dtype),
        grid_spec=grid_spec,
        compiler_params=pltpu.CompilerParams(vmem_limit_bytes=VMEM_LIMIT),
        name="cycles",
    )(spot, ranks, *[arrived] * (LEFT + RIGHT), projectors, amplitudes)


def update_kernel(spot, ranks, orbitals, levels, *refs):
    count = LEFT + RIGHT
    slabs, sums = refs[:count], refs[count : 2 * count]
    projectors, energies, out, left, right, left_sum, right_sum = refs[2 * count :]
    tile = pl.program_id(0)
    turned = [value.T for value in masked_blocks(ranks, projectors, tile)]
    project(turned, slabs, left, right)
    project(turned, sums, left_sum, right_sum)
    across = (((1,), (1,)), ((), ()))

    def product(a, b):
        return lax.dot_general(a, b, across, preferred_element_type=jnp.float32)

    for pair in range(PAIRS_TILE):
        residual = product(left[pair], right[pair])
        residual = residual + product(left[pair], right_sum[pair])
        residual = residual + product(left_sum[pair], right[pair])
        along = jnp.broadcast_to(energies[0, pair : pair + 1], residual.shape)
        gap = along.T + along
        gap = gap + levels[orbitals[tile * count + pair // RIGHT]]
        gap = gap + levels[orbitals[tile * count + LEFT + pair % RIGHT]]
        rank = ranks[tile * PAIRS_TILE + pair]
        kept = lax.broadcasted_iota(jnp.int32, residual.shape, 0) < rank
        kept = kept & (lax.broadcasted_iota(jnp.int32, residual.shape, 1) < rank)
        out[pair] = jnp.where(kept, -residual / gap, 0.0)


def update(spot, ranks, orbitals, levels, arrived, returned, projectors, pair_energies):
    slab = arrived.shape[1:]
    wide = projectors.shape[2]
    tiles = projectors.shape[0] // PAIRS_TILE
    held = pltpu.VMEM((PAIRS_TILE, wide, slab[1]), arrived.dtype)
    grid_spec = pltpu.PrefetchScalarGridSpec(
        num_scalar_prefetch=4,
        grid=(tiles,),
        in_specs=slab_specs(slab)
        + slab_specs(slab)
        + [
            pl.BlockSpec((PAIRS_TILE,) + projectors.shape[1:], lambda tile, *_: (tile, 0, 0)),
            pl.BlockSpec((1, PAIRS_TILE, wide), lambda tile, *_: (tile, 0, 0)),
        ],
        out_specs=pl.BlockSpec((PAIRS_TILE, wide, wide), lambda tile, *_: (tile, 0, 0)),
        scratch_shapes=[held] * 4,
    )
    count = LEFT + RIGHT
    return pl.pallas_call(
        update_kernel,
        out_shape=jax.ShapeDtypeStruct((tiles * PAIRS_TILE, wide, wide), jnp.float32),
        grid_spec=grid_spec,
        compiler_params=pltpu.CompilerParams(vmem_limit_bytes=VMEM_LIMIT),
        name="update",
    )(
        spot,
        ranks,
        orbitals,
        levels,
        *[arrived] * count,
        *[returned] * count,
        projectors,
        pair_energies.reshape(tiles, PAIRS_TILE, wide),
    )


def body(
    factors,
    orbital_owner,
    tile_orbitals,
    projectors,
    amplitudes,
    ranks,
    pair_energies,
    orbital_energies,
):
    dev_count = lax.axis_size("dev")
    planes = planes_of(dev_count)
    width = dev_count // planes
    tile_count = tile_orbitals.shape[0]
    orb_count, factor_width, aux_width = factors.shape
    need_count = tile_count * 7
    slots = -(-(8 * tile_count) // dev_count)
    my_orbitals = tile_orbitals.reshape(need_count)
    owner = orbital_owner[my_orbitals]
    entry = jnp.arange(need_count)
    same = (owner[:, None] == owner[None, :]) & (entry[None, :] < entry[:, None])
    slot = jnp.sum(same.astype(jnp.int32), axis=1)
    spot = lax.rem(owner, width) * (planes * slots) + lax.div(owner, width) * slots + slot
    hit = spot[None, :] == jnp.arange(dev_count * slots)[:, None]
    row_at = jnp.sum(jnp.where(hit, lax.div(my_orbitals, dev_count)[None, :] + 1, 0), axis=1) - 1
    want = jnp.zeros((width, 8, 128), jnp.int32)
    want = want.at[:, 0, : planes * slots].set(row_at.reshape(width, planes * slots))
    asked = ask(want, planes)[:, 0, : planes * slots]
    picks = jnp.maximum(asked, 0)
    by_plane = asked.reshape(width, planes, slots).transpose(1, 0, 2)
    match = by_plane[:, None] == jnp.arange(orb_count)[None, :, None, None]
    slot_code = jnp.arange(width * slots).reshape(width, slots)
    table = jnp.sum(jnp.where(match, slot_code + 1, 0), axis=3) - 1
    table = table.reshape(planes * orb_count, width)
    arrived = fetch(factors, picks, planes, slots, 2)
    arrived = arrived.reshape(dev_count * slots, factor_width, aux_width)
    outgoing = cycles(spot, ranks, arrived, projectors, amplitudes)
    outgoing = outgoing.reshape(width, planes * slots, factor_width, aux_width)
    orbital_sums = reduce_slots(outgoing, table, orb_count, planes, slots)
    returned = fetch(orbital_sums, picks, planes, slots, 4)
    returned = returned.reshape(dev_count * slots, factor_width, aux_width)
    updated = update(
        spot, ranks, my_orbitals, orbital_energies, arrived, returned, projectors, pair_energies
    )
    return (updated, orbital_sums)


def solution(mesh):
    in_specs = (
        P("dev", None, None),
        P(),
        P("dev", None),
        P("dev", None, None),
        P("dev", None, None),
        P("dev"),
        P("dev", None),
        P(),
    )
    out_specs = (P("dev", None, None), P("dev", None, None))
    return jax.shard_map(body, mesh=mesh, in_specs=in_specs, out_specs=out_specs, check_vma=False)
```

```python
import functools
import math
import jax
import jax.numpy as jnp
from jax import lax
from jax.experimental import pallas as pl
from jax.experimental.pallas import tpu as pltpu
from jax.sharding import PartitionSpec as P

PLANES = 4
MESH = pl.DeviceIdType.MESH
VMEM_LIMIT = 60 << 20


def planes_of(dev_count):
    return math.gcd(PLANES, dev_count)


def place(planes):
    width = lax.axis_size("dev") // planes
    me = lax.axis_index("dev")
    return me, lax.div(me, width), lax.rem(me, width), width


def greet(barrier, me, z, col, planes, width, lines):
    base = z * width

    @pl.loop(1, width)
    def _(step):
        peer = base + lax.rem(col + step, width)
        pl.semaphore_signal(barrier, inc=1, device_id=(peer,), device_id_type=MESH)

    count = width - 1
    if lines:

        @pl.when(z > 0)
        def _():
            pl.semaphore_signal(barrier, inc=1, device_id=(me - width,), device_id_type=MESH)

        @pl.when(z < planes - 1)
        def _():
            pl.semaphore_signal(barrier, inc=1, device_id=(me + width,), device_id_type=MESH)

        count = count + jnp.where(z > 0, 1, 0) + jnp.where(z < planes - 1, 1, 0)

    pl.semaphore_wait(barrier, count)


def fetch_kernel(planes, slots, want, source, out, got, mine, picks, local, ask_send, ask_recv, *scratch):
    me, z, col, width = place(planes)
    load = pltpu.make_async_copy(source, mine, local.at[0])
    load.start()
    greet(pltpu.get_barrier_semaphore(), me, z, col, planes, width, True)

    def asking(peer, home):
        return pltpu.make_async_remote_copy(
            src_ref=want.at[peer],
            dst_ref=got.at[home],
            send_sem=ask_send.at[peer],
            recv_sem=ask_recv.at[home],
            device_id=(z * width + peer,),
            device_id_type=MESH,
        )

    @pl.loop(1, width)
    def _(step):
        asking(lax.rem(col + step, width), col).start()

    got[col] = want[col]

    def ready():
        @pl.loop(1, width)
        def _(step):
            peer = lax.rem(col + step, width)
            asking(peer, peer).wait_recv()
            asking(peer, peer).wait_send()

        table = pltpu.make_async_copy(got, picks, local.at[1])
        table.start()
        table.wait()
        load.wait()

    def pick(peer, at):
        return jnp.maximum(picks[peer, 0, at], 0)

    spread(planes, slots, pick, source, out, mine, ready, scratch, True)


def spread(planes, slots, pick, source, out, mine, ready, scratch, early=False):
    below, above = scratch[: planes - 1], scratch[planes - 1 : 2 * planes - 2]
    pack, line_send, line_recv, send, recv, keep = scratch[2 * planes - 2 :]
    me, z, col, width = place(planes)

    def hop(way, dist):
        held = below if way == 0 else above
        return pltpu.make_async_remote_copy(
            src_ref=source if dist == 0 else held[dist - 1],
            dst_ref=held[dist],
            send_sem=line_send.at[way, dist],
            recv_sem=line_recv.at[way, dist],
            device_id=(me + width if way == 0 else me - width,),
            device_id_type=MESH,
        )

    def onward(way):
        return z < planes - 1 if way == 0 else z > 0

    def there(way, dist):
        return z - dist >= 0 if way == 0 else z + dist < planes

    def sent(peer, block, home):
        span = pl.ds(block * slots, slots)
        return pltpu.make_async_remote_copy(
            src_ref=pack.at[peer, span],
            dst_ref=out.at[home, span],
            send_sem=send.at[peer, block],
            recv_sem=recv.at[home, block],
            device_id=(z * width + peer,),
            device_id_type=MESH,
        )

    def kept(block):
        span = pl.ds(block * slots, slots)
        return pltpu.make_async_copy(pack.at[col, span], out.at[col, span], keep.at[block])

    def serve(held, block, depart=None):
        @pl.loop(0, width)
        def _(step):
            peer = lax.rem(col + step, width)
            for slot in range(slots):
                at = block * slots + slot
                pack[peer, at] = held[pick(peer, at)]

        if depart is not None:
            depart()

        @pl.loop(1, width)
        def _(step):
            sent(lax.rem(col + step, width), block, col).start()

        kept(block).start()

    def depart():
        for way in range(2):
            if planes > 1:

                @pl.when(onward(way))
                def _():
                    hop(way, 0).start()

    if early:
        depart()
    ready()
    serve(mine, z, None if early else depart)
    for dist in range(1, planes):
        for way in range(2):

            @pl.when(there(way, dist))
            def _():
                hop(way, dist - 1).wait_recv()
                if dist < planes - 1:

                    @pl.when(onward(way))
                    def _():
                        hop(way, dist).start()

                serve((below if way == 0 else above)[dist - 1], z - dist if way == 0 else z + dist)

    for dist in range(planes - 1):
        for way in range(2):

            @pl.when(onward(way) & there(way, dist))
            def _():
                hop(way, dist).wait_send()

    @pl.loop(0, planes)
    def _(block):
        @pl.loop(1, width)
        def _(step):
            peer = lax.rem(col + step, width)
            sent(peer, block, peer).wait_recv()
            sent(peer, block, peer).wait_send()

        kept(block).wait()


def spread_scratch(shape, kind, planes, slots, width):
    return [pltpu.VMEM(shape, kind)] * (2 * planes - 2) + [
        pltpu.VMEM((width, planes * slots) + shape[1:], kind),
        pltpu.SemaphoreType.DMA((2, planes)),
        pltpu.SemaphoreType.DMA((2, planes)),
        pltpu.SemaphoreType.DMA((width, planes)),
        pltpu.SemaphoreType.DMA((width, planes)),
        pltpu.SemaphoreType.DMA((planes,)),
    ]


def fetch(source, want, planes, slots):
    width = want.shape[0]
    slab = source.shape[1:]
    return pl.pallas_call(
        functools.partial(fetch_kernel, planes, slots),
        out_shape=(
            jax.ShapeDtypeStruct((width, planes * slots) + slab, source.dtype),
            jax.ShapeDtypeStruct(want.shape, want.dtype),
        ),
        in_specs=[
            pl.BlockSpec(memory_space=pltpu.VMEM),
            pl.BlockSpec(memory_space=pl.ANY),
        ],
        out_specs=(
            pl.BlockSpec(memory_space=pl.ANY),
            pl.BlockSpec(memory_space=pltpu.VMEM),
        ),
        scratch_shapes=[
            pltpu.VMEM(source.shape, source.dtype),
            pltpu.SMEM(want.shape, want.dtype),
            pltpu.SemaphoreType.DMA((2,)),
            pltpu.SemaphoreType.DMA((width,)),
            pltpu.SemaphoreType.DMA((width,)),
        ]
        + spread_scratch(source.shape, source.dtype, planes, slots, width),
        compiler_params=pltpu.CompilerParams(
            collective_id=2, has_side_effects=True, vmem_limit_bytes=VMEM_LIMIT
        ),
        name="fetch",
    )(want, source)


def farthest_first(planes, z, turn):
    block = 0
    for own in range(planes):
        order = sorted(range(planes), key=lambda b: (-abs(b - own), b))
        block = block + jnp.where(z == own, order[turn], 0)
    return block


def row_chunk(rows):
    return next(size for size in (64, 48, 32, 16, 8, rows) if rows % size == 0)


def reduce_kernel(planes, slots, table, picks, outgoing, out, returned, *scratch):
    landed = scratch[:planes]
    total, inbox, outbox, send, recv, keep, line_send, line_recv = scratch[planes : planes + 8]
    me, z, col, width = place(planes)
    orbs, rows = total.shape[:2]
    chunk = row_chunk(rows)
    greet(pltpu.get_barrier_semaphore(), me, z, col, planes, width, True)

    def sent(peer, turn, home):
        span = pl.ds(farthest_first(planes, z, turn) * slots, slots)
        return pltpu.make_async_remote_copy(
            src_ref=outgoing.at[peer, span],
            dst_ref=landed[turn].at[pl.ds(home * slots, slots)],
            send_sem=send.at[peer, turn],
            recv_sem=recv.at[home, turn],
            device_id=(z * width + peer,),
            device_id_type=MESH,
        )

    def kept(turn):
        span = pl.ds(farthest_first(planes, z, turn) * slots, slots)
        return pltpu.make_async_copy(
            outgoing.at[col, span], landed[turn].at[pl.ds(col * slots, slots)], keep.at[turn]
        )

    def hop(way, block):
        return pltpu.make_async_remote_copy(
            src_ref=outbox.at[block],
            dst_ref=inbox.at[way, block],
            send_sem=line_send.at[block],
            recv_sem=line_recv.at[way, block],
            device_id=(me + width if way == 0 else me - width,),
            device_id_type=MESH,
        )

    for turn in range(planes):

        @pl.loop(1, width)
        def _(step):
            sent(lax.rem(col + step, width), turn, col).start()

        kept(turn).start()

    def add_line(way, block):
        hop(way, block).wait_recv()

        @pl.loop(0, orbs)
        def _(orb):
            for first in range(0, rows, chunk):
                part = pl.ds(first, chunk)
                total[orb, part] += inbox[way, block, orb, part].astype(jnp.float32)

    for turn in range(planes):
        block = farthest_first(planes, z, turn)

        @pl.loop(1, width)
        def _(step):
            peer = lax.rem(col + step, width)
            sent(peer, turn, peer).wait_recv()

        kept(turn).wait()

        @pl.loop(0, orbs)
        def _(orb):
            for first in range(0, rows, chunk):
                part = pl.ds(first, chunk)
                value = jnp.zeros((chunk, total.shape[2]), jnp.float32)
                for source in range(width):
                    at = table[block * orbs + orb, source]
                    slab = landed[turn][jnp.maximum(at, 0), part].astype(jnp.float32)
                    value = value + jnp.where(at >= 0, slab, 0.0)
                total[orb, part] = value

        if turn < planes - 1:
            for way in range(2):

                @pl.when(block > z if way == 0 else block < z)
                def _():
                    @pl.when(z > 0 if way == 0 else z < planes - 1)
                    def _():
                        add_line(way, block)

                    outbox[block] = total[...].astype(outbox.dtype)
                    hop(way, block).start()

        else:

            @pl.when(z > 0)
            def _():
                add_line(0, z)

            @pl.when(z < planes - 1)
            def _():
                add_line(1, z)

            out[...] = total[...].astype(out.dtype)

    for turn in range(planes):
        if turn < planes - 1:
            hop(0, farthest_first(planes, z, turn)).wait_send()

        @pl.loop(1, width)
        def _(step):
            sent(lax.rem(col + step, width), turn, col).wait_send()

    def pick(peer, at):
        return picks[peer, at]

    spread(planes, slots, pick, out, returned, out, lambda: None, scratch[planes + 8 :])


def reduce_slots(outgoing, table, picks, orbs, planes, slots):
    width = outgoing.shape[0]
    slab = outgoing.shape[2:]
    kind = outgoing.dtype
    return pl.pallas_call(
        functools.partial(reduce_kernel, planes, slots),
        out_shape=(
            jax.ShapeDtypeStruct((orbs,) + slab, kind),
            jax.ShapeDtypeStruct(outgoing.shape, kind),
        ),
        in_specs=[
            pl.BlockSpec(memory_space=pltpu.SMEM),
            pl.BlockSpec(memory_space=pltpu.SMEM),
            pl.BlockSpec(memory_space=pl.ANY),
        ],
        out_specs=(
            pl.BlockSpec(memory_space=pltpu.VMEM),
            pl.BlockSpec(memory_space=pl.ANY),
        ),
        scratch_shapes=[pltpu.VMEM((width * slots,) + slab, kind)] * planes
        + [
            pltpu.VMEM((orbs,) + slab, jnp.float32),
            pltpu.VMEM((2, planes, orbs) + slab, kind),
            pltpu.VMEM((planes, orbs) + slab, kind),
            pltpu.SemaphoreType.DMA((width, planes)),
            pltpu.SemaphoreType.DMA((width, planes)),
            pltpu.SemaphoreType.DMA((planes,)),
            pltpu.SemaphoreType.DMA((planes,)),
            pltpu.SemaphoreType.DMA((2, planes)),
        ]
        + spread_scratch((orbs,) + slab, kind, planes, slots, width),
        compiler_params=pltpu.CompilerParams(
            collective_id=3, has_side_effects=True, vmem_limit_bytes=VMEM_LIMIT
        ),
        name="reduce_slots",
    )(table, picks, outgoing)


LEFT, RIGHT = 4, 3
PAIRS_TILE = LEFT * RIGHT


def masked_blocks(ranks, projectors, tile):
    kept = []
    for pair in range(PAIRS_TILE):
        value = projectors[pair]
        lane = lax.broadcasted_iota(jnp.int32, value.shape, 1)
        kept.append(jnp.where(lane < ranks[tile * PAIRS_TILE + pair], value, jnp.zeros_like(value)))
    return kept


def project(turned, slabs, left_out, right_out):
    width = turned[0].shape[0]
    for a in range(LEFT):
        stack = jnp.concatenate([turned[RIGHT * a + b] for b in range(RIGHT)], axis=0)
        value = jnp.dot(stack, slabs[a][0], preferred_element_type=jnp.float32)
        value = value.astype(left_out.dtype)
        for b in range(RIGHT):
            left_out[RIGHT * a + b] = value[b * width : (b + 1) * width]
    for b in range(RIGHT):
        stack = jnp.concatenate([turned[RIGHT * a + b] for a in range(LEFT)], axis=0)
        value = jnp.dot(stack, slabs[LEFT + b][0], preferred_element_type=jnp.float32)
        value = value.astype(right_out.dtype)
        for a in range(LEFT):
            right_out[RIGHT * a + b] = value[a * width : (a + 1) * width]


def cycle_kernel(spot, ranks, *refs):
    slabs = refs[: LEFT + RIGHT]
    projectors, amplitudes, out, left, right, staged, sems = refs[LEFT + RIGHT :]
    tile = pl.program_id(0)
    half = lax.rem(tile, 2)

    def put(at, which, entry):
        target = out.at[spot[at * (LEFT + RIGHT) + entry]]
        return pltpu.make_async_copy(staged.at[which, entry], target, sems.at[which, entry])

    kept = masked_blocks(ranks, projectors, tile)
    project([value.T for value in kept], slabs, left, right)
    for pair in range(PAIRS_TILE):
        amp = amplitudes[pair].astype(jnp.bfloat16)
        from_right = jnp.dot(amp, right[pair], preferred_element_type=jnp.float32)
        from_left = jnp.dot(amp.T, left[pair], preferred_element_type=jnp.float32)
        left[pair] = from_right.astype(left.dtype)
        right[pair] = from_left.astype(right.dtype)

    @pl.when(tile >= 2)
    def _():
        for entry in range(LEFT + RIGHT):
            put(tile - 2, half, entry).wait()

    for entry in range(LEFT + RIGHT):
        if entry < LEFT:
            pairs, cycles = [RIGHT * entry + b for b in range(RIGHT)], left
        else:
            pairs, cycles = [RIGHT * a + entry - LEFT for a in range(LEFT)], right
        wide = jnp.concatenate([kept[pair] for pair in pairs], axis=1)
        tall = jnp.concatenate([cycles[pair] for pair in pairs], axis=0)
        value = jnp.dot(wide, tall, preferred_element_type=jnp.float32)
        staged[half, entry] = value.astype(staged.dtype)
        put(tile, half, entry).start()

    @pl.when(tile == pl.num_programs(0) - 1)
    def _():
        for entry in range(LEFT + RIGHT):
            put(tile, half, entry).wait()

        @pl.when(tile >= 1)
        def _():
            for entry in range(LEFT + RIGHT):
                put(tile - 1, 1 - half, entry).wait()


def slab_specs(slab):
    def at(entry):
        return lambda tile, spot, *_: (spot[tile * (LEFT + RIGHT) + entry], 0, 0)

    return [pl.BlockSpec((1,) + slab, at(entry)) for entry in range(LEFT + RIGHT)]


def cycles(spot, ranks, arrived, projectors, amplitudes):
    slab = arrived.shape[1:]
    wide = projectors.shape[2]
    held = pltpu.VMEM((PAIRS_TILE, wide, slab[1]), arrived.dtype)
    grid_spec = pltpu.PrefetchScalarGridSpec(
        num_scalar_prefetch=2,
        grid=(projectors.shape[0] // PAIRS_TILE,),
        in_specs=slab_specs(slab)
        + [
            pl.BlockSpec((PAIRS_TILE,) + projectors.shape[1:], lambda tile, *_: (tile, 0, 0)),
            pl.BlockSpec((PAIRS_TILE,) + amplitudes.shape[1:], lambda tile, *_: (tile, 0, 0)),
        ],
        out_specs=pl.BlockSpec(memory_space=pl.ANY),
        scratch_shapes=[
            held,
            held,
            pltpu.VMEM((2, LEFT + RIGHT) + slab, arrived.dtype),
            pltpu.SemaphoreType.DMA((2, LEFT + RIGHT)),
        ],
    )
    return pl.pallas_call(
        cycle_kernel,
        out_shape=jax.ShapeDtypeStruct(arrived.shape, arrived.dtype),
        grid_spec=grid_spec,
        compiler_params=pltpu.CompilerParams(vmem_limit_bytes=VMEM_LIMIT),
        name="cycles",
    )(spot, ranks, *[arrived] * (LEFT + RIGHT), projectors, amplitudes)


def update_kernel(spot, ranks, orbitals, levels, *refs):
    count = LEFT + RIGHT
    slabs, sums = refs[:count], refs[count : 2 * count]
    projectors, energies, out, left, right, left_sum, right_sum = refs[2 * count :]
    tile = pl.program_id(0)
    turned = [value.T for value in masked_blocks(ranks, projectors, tile)]
    project(turned, slabs, left, right)
    project(turned, sums, left_sum, right_sum)
    across = (((1,), (1,)), ((), ()))

    def product(a, b):
        return lax.dot_general(a, b, across, preferred_element_type=jnp.float32)

    for pair in range(PAIRS_TILE):
        residual = product(left[pair], right[pair])
        residual = residual + product(left[pair], right_sum[pair])
        residual = residual + product(left_sum[pair], right[pair])
        own = energies[pl.ds(tile * PAIRS_TILE + pair, 1)]
        along = jnp.broadcast_to(own, residual.shape)
        gap = along.T + along
        gap = gap + levels[orbitals[tile * count + pair // RIGHT]]
        gap = gap + levels[orbitals[tile * count + LEFT + pair % RIGHT]]
        rank = ranks[tile * PAIRS_TILE + pair]
        kept = lax.broadcasted_iota(jnp.int32, residual.shape, 0) < rank
        kept = kept & (lax.broadcasted_iota(jnp.int32, residual.shape, 1) < rank)
        out[pair] = jnp.where(kept, -residual / gap, 0.0)


def update(spot, ranks, orbitals, levels, arrived, returned, projectors, pair_energies):
    slab = arrived.shape[1:]
    wide = projectors.shape[2]
    tiles = projectors.shape[0] // PAIRS_TILE
    held = pltpu.VMEM((PAIRS_TILE, wide, slab[1]), arrived.dtype)
    grid_spec = pltpu.PrefetchScalarGridSpec(
        num_scalar_prefetch=4,
        grid=(tiles,),
        in_specs=slab_specs(slab)
        + slab_specs(slab)
        + [
            pl.BlockSpec((PAIRS_TILE,) + projectors.shape[1:], lambda tile, *_: (tile, 0, 0)),
            pl.BlockSpec(pair_energies.shape, lambda tile, *_: (0, 0)),
        ],
        out_specs=pl.BlockSpec((PAIRS_TILE, wide, wide), lambda tile, *_: (tile, 0, 0)),
        scratch_shapes=[held] * 4,
    )
    count = LEFT + RIGHT
    return pl.pallas_call(
        update_kernel,
        out_shape=jax.ShapeDtypeStruct((tiles * PAIRS_TILE, wide, wide), jnp.float32),
        grid_spec=grid_spec,
        compiler_params=pltpu.CompilerParams(vmem_limit_bytes=VMEM_LIMIT),
        name="update",
    )(
        spot,
        ranks,
        orbitals,
        levels,
        *[arrived] * count,
        *[returned] * count,
        projectors,
        pair_energies,
    )


def body(
    factors,
    orbital_owner,
    tile_orbitals,
    projectors,
    amplitudes,
    ranks,
    pair_energies,
    orbital_energies,
):
    dev_count = lax.axis_size("dev")
    planes = planes_of(dev_count)
    width = dev_count // planes
    tile_count = tile_orbitals.shape[0]
    orb_count, factor_width, aux_width = factors.shape
    need_count = tile_count * 7
    slots = -(-(8 * tile_count) // dev_count)
    my_orbitals = tile_orbitals.reshape(need_count)
    owner = orbital_owner[my_orbitals]
    entry = jnp.arange(need_count)
    same = (owner[:, None] == owner[None, :]) & (entry[None, :] < entry[:, None])
    slot = jnp.sum(same.astype(jnp.int32), axis=1)
    spot = lax.rem(owner, width) * (planes * slots) + lax.div(owner, width) * slots + slot
    hit = spot[None, :] == jnp.arange(dev_count * slots)[:, None]
    row_at = jnp.sum(jnp.where(hit, lax.div(my_orbitals, dev_count)[None, :] + 1, 0), axis=1) - 1
    want = jnp.zeros((width, 8, 128), jnp.int32)
    want = want.at[:, 0, : planes * slots].set(row_at.reshape(width, planes * slots))
    arrived, asked = fetch(factors, want, planes, slots)
    asked = asked[:, 0, : planes * slots]
    picks = jnp.maximum(asked, 0)
    by_plane = asked.reshape(width, planes, slots).transpose(1, 0, 2)
    match = by_plane[:, None] == jnp.arange(orb_count)[None, :, None, None]
    slot_code = jnp.arange(width * slots).reshape(width, slots)
    table = jnp.sum(jnp.where(match, slot_code + 1, 0), axis=3) - 1
    table = table.reshape(planes * orb_count, width)
    arrived = arrived.reshape(dev_count * slots, factor_width, aux_width)
    outgoing = cycles(spot, ranks, arrived, projectors, amplitudes)
    outgoing = outgoing.reshape(width, planes * slots, factor_width, aux_width)
    orbital_sums, returned = reduce_slots(outgoing, table, picks, orb_count, planes, slots)
    returned = returned.reshape(dev_count * slots, factor_width, aux_width)
    updated = update(
        spot, ranks, my_orbitals, orbital_energies, arrived, returned, projectors, pair_energies
    )
    return (updated, orbital_sums)


def solution(mesh):
    in_specs = (
        P("dev", None, None),
        P(),
        P("dev", None),
        P("dev", None, None),
        P("dev", None, None),
        P("dev"),
        P("dev", None),
        P(),
    )
    out_specs = (P("dev", None, None), P("dev", None, None))
    return jax.shard_map(body, mesh=mesh, in_specs=in_specs, out_specs=out_specs, check_vma=False)
```
